512 devices in a mesh: seq: 32 (over x, y), grp: 16 (over z, core).
Axes of the slice: x: 4, y: 8, z: 8, core: 2. Of those that a mesh axis runs over, the one named last changes fastest.
Arguments:
- normed_hidden_input: bfloat16 [65536, 4096], P(('grp', 'seq')), may hold values from -6 to 6
- frozen_query_rows: bfloat16 [65536, 4096], P(('grp', 'seq')), may hold values from -16 to 16
- frozen_key_rows: bfloat16 [65536, 1024], P(('grp', 'seq')), may hold values from -16 to 16
- attention_output_gradient: bfloat16 [65536, 4096], P(('grp', 'seq')), may hold values from -0.15625 to 0.15625
- adapter_down_weight: bfloat16 [256, 64, 4096], P('grp', None, 'seq'), may hold values from -0.09375 to 0.09375
- adapter_up_weight: bfloat16 [256, 64, 1024], P('grp', 'seq'), may hold values from -0.75 to 0.75
- segment_adapter_index: int32 [16, 16], replicated, may hold values from 0 to 255, as said below
- segment_block_count: int32 [16, 16], replicated, may hold values from 1 to 16, 32 in all within a row
- adapter_row_index: int32 [256], replicated, may hold values from 0 to 255, as said below
Outputs:
- down_grad: float32 [256, 64, 4096], P('grp', None, 'seq')
- up_grad: float32 [256, 64, 1024], P('grp', 'seq')
The draws below stay inside these ranges and needn't reach their ends.
Inputs may be any that keep to these rules, and one draw needn't show every extreme that they name: A permutation: adapter a is held in row adapter_row_index[a] of adapter_down_weight and adapter_up_weight. `segment_adapter_index`: call rows g * 16 to (g + 1) * 16 - 1 of adapter_down_weight the rows of index g of grp. In each sequence at most 2 segments use adapters held in the rows of one index of grp, and in every sequence some index holds exactly 2 of them. Tenants may repeat within and across sequences. `segment_block_count`: each row sums to 32; in each row some segment has exactly 16 blocks.
All inputs are finite; a program needn't handle non-finite values.
Results may differ from the reference program's by a relative error of at most 0.0056.
Values may be sent and summed in bfloat16 or wider, within the bound.
No kernel may reach another device: no remote copies, remote signals or barrier semaphores. Data moves between devices by JAX's collectives and lax.ppermute only.
A program may use at most 64 MiB of HBM per device.

```python
import math
import jax
import jax.numpy as jnp
import numpy as np
from jax import lax

MODEL_WIDTH = 4096
HEADS = 32
KV_HEADS = 8
HEAD_DIM = 128
ADAPTER_RANK = 64
BLOCK = 128
QROWS = 512
TOK_DEV = 128
ADAPT_GRP = 16
SEQLEN = 4096
TOKENS = 65536
ADAPTER_COUNT = 256
VALUE_WIDTH = 1024
SEGS = 16
MOSTBLK = 16
CAP = 2
N_SEQ = 32
N_GRP = 16


def draw_frozen_key_rows(key, part):
    base_key = jax.random.fold_in(key, 2)
    base = jnp.clip(jax.random.normal(base_key, (TOKENS, KV_HEADS * HEAD_DIM)), -6.0, 6.0)
    return base.astype(jnp.bfloat16)


def draw_frozen_query_rows(key, part):
    base_key = jax.random.fold_in(key, 1)
    base = jnp.clip(jax.random.normal(base_key, (TOKENS, HEADS * HEAD_DIM)), -6.0, 6.0)
    return base.astype(jnp.bfloat16)


def tenant_layout(key):
    groups = ADAPTER_COUNT // ADAPT_GRP
    owner = jax.random.permutation(jax.random.fold_in(key, 31), ADAPTER_COUNT).astype(jnp.int32)
    inverse = jnp.zeros((ADAPTER_COUNT,), jnp.int32).at[owner].set(jnp.arange(ADAPTER_COUNT, dtype=jnp.int32))

    def one_sequence(seq_key):
        full_key, order_key, shuffle_key, local_key = jax.random.split(seq_key, 4)
        full_group = jax.random.randint(full_key, (), 0, groups)
        pool = jnp.arange(groups * CAP, dtype=jnp.int32) // CAP
        scores = jax.random.permutation(order_key, groups * CAP).astype(jnp.int32)
        scores = jnp.where(pool == full_group, -1, scores)
        picked = pool[jnp.argsort(scores, stable=True)[:SEGS]]
        picked = picked[jax.random.permutation(shuffle_key, SEGS)]
        slots = picked * ADAPT_GRP + jax.random.randint(local_key, (SEGS,), 0, ADAPT_GRP)
        return inverse[slots]
    seq_keys = jax.random.split(jax.random.fold_in(key, 32), groups)
    tenants = jax.vmap(one_sequence)(seq_keys).astype(jnp.int32)
    return (owner, tenants)


def draw_adapter_row_index(key, part):
    owner, tenants = tenant_layout(key)
    return owner


def draw_segment_adapter_index(key, part):
    owner, tenants = tenant_layout(key)
    return tenants


def block_scale(stream_key, shape, cuts, low, largest):
    loudness, own = 1.0, jax.random.fold_in(stream_key, 6)
    for dim, blocks in cuts:
        steps = jnp.exp(jax.random.uniform(jax.random.fold_in(own, dim), (blocks,), jnp.float32, low / len(cuts), largest / len(cuts)))
        loudness = loudness * jnp.repeat(steps, shape[dim] // blocks).reshape([-1 if axis == dim else 1 for axis in range(len(shape))])
    return loudness


def split_up(count, total, most, skew):
    loads = [(1 << 20) // math.isqrt(grade ** skew) + 1 for grade in range(2, count + 1)]
    spare, given = total - most - (count - 1), [1] * (count - 1)
    while spare > 0:
        candidates = [i for i in range(count - 1) if given[i] < most]
        whole, remaining = sum([loads[i] for i in candidates]), spare
        for i in candidates:
            extra = min(most - given[i], max(1, remaining * loads[i] // whole), spare)
            given[i] = given[i] + extra
            spare = spare - extra
    return np.array([most] + given)


def ragged_sizes(own_key, number_of, total, limit, slope):
    if number_of == 2:
        one = jax.random.randint(own_key, (), max(1, total - limit), min(limit, total - 1) + 1)
        return jnp.stack([one, total - one])
    lengths = jnp.asarray(split_up(number_of, total, limit, slope), jnp.int32)
    pairs = (number_of - 1) // 2
    donor, receiver = lengths[1:1 + 2 * pairs:2], lengths[2:2 + 2 * pairs:2]
    slack = jnp.minimum(donor - 1, limit - receiver)
    moved = jax.random.randint(jax.random.fold_in(own_key, 1), (pairs,), 0, 1 << 20) % (slack + 1)
    lengths = lengths.at[1:1 + 2 * pairs:2].set(donor - moved).at[2:2 + 2 * pairs:2].set(receiver + moved)
    return lengths[jax.random.permutation(jax.random.fold_in(own_key, 2), number_of)]


def noise(key, shape, deviation, bound, pieces=(), held_as=jnp.bfloat16):
    array = deviation * jax.random.normal(key, shape, jnp.float32)
    if pieces:
        array = array * block_scale(key, shape, pieces, -0.22, 0.18)
    return jnp.clip(array, -bound, bound).astype(held_as)


def setup_inputs(seed: int = 0) -> dict:
    key_list = jax.random.split(jax.random.key(seed), 10)
    normed_hidden_input = noise(key_list[0], (TOKENS, MODEL_WIDTH), 1.0, 6.0, ((0, 512),))
    frozen_query_rows = draw_frozen_query_rows(jax.random.fold_in(key_list[9], 71), 0)
    frozen_key_rows = draw_frozen_key_rows(jax.random.fold_in(key_list[9], 71), 0)
    attention_output_gradient = noise(key_list[3], (TOKENS, HEADS * HEAD_DIM), 0.01, 0.15625, ((0, 512),))
    adapter_down_weight = noise(key_list[4], (ADAPTER_COUNT, ADAPTER_RANK, MODEL_WIDTH), MODEL_WIDTH ** -0.5, 0.09375, ((0, 16), (2, 32)))
    adapter_up_weight = noise(key_list[5], (ADAPTER_COUNT, ADAPTER_RANK, VALUE_WIDTH), ADAPTER_RANK ** -0.5, 0.75, ((0, 16), (1, 32)))
    segment_adapter_index = draw_segment_adapter_index(jax.random.fold_in(key_list[9], 71), 0)
    segment_block_count = jax.vmap(lambda own: ragged_sizes(own, SEGS, N_SEQ * TOK_DEV // BLOCK, MOSTBLK, 2))(jax.random.split(key_list[7], N_GRP)).reshape((N_GRP, SEGS)).astype(jnp.int32)
    adapter_row_index = draw_adapter_row_index(jax.random.fold_in(key_list[9], 71), 0)
    return {"normed_hidden_input": normed_hidden_input, "frozen_query_rows": frozen_query_rows, "frozen_key_rows": frozen_key_rows, "attention_output_gradient": attention_output_gradient, "adapter_down_weight": adapter_down_weight, "adapter_up_weight": adapter_up_weight, "segment_adapter_index": segment_adapter_index, "segment_block_count": segment_block_count, "adapter_row_index": adapter_row_index}


adapter_scale = 2.0

def attend_head(query_head, key_head, grad_head, segment_ids, query_rows, reach):
    length, head_width = query_head.shape
    padded_keys = jnp.concatenate([jnp.zeros((reach, head_width), key_head.dtype), key_head], 0)
    padded_ids = jnp.concatenate([jnp.full((reach,), -1, jnp.int32), segment_ids.astype(jnp.int32)], 0)
    window = query_rows + reach
    factor = 1.0 / math.sqrt(head_width)

    def one_block(totals, number):
        offset = number * query_rows
        query_block = lax.dynamic_slice_in_dim(query_head, offset, query_rows, 0)
        grad_block = lax.dynamic_slice_in_dim(grad_head, offset, query_rows, 0)
        key_block = lax.dynamic_slice_in_dim(padded_keys, offset, window, 0)
        key_ids = lax.dynamic_slice_in_dim(padded_ids, offset, window, 0)
        query_ids = lax.dynamic_slice_in_dim(segment_ids.astype(jnp.int32), offset, query_rows, 0)
        scores = jnp.dot(query_block, key_block.T, preferred_element_type=jnp.float32) * factor
        query_pos = offset + jnp.arange(query_rows, dtype=jnp.int32)
        key_pos = offset - reach + jnp.arange(window, dtype=jnp.int32)
        allowed = (key_ids[None, :] == query_ids[:, None]) & (key_pos[None, :] <= query_pos[:, None])
        scores = jnp.where(allowed, scores, jnp.float32(-1e+30))
        highest = lax.optimization_barrier(jnp.max(scores, axis=1, keepdims=True))
        expo = jnp.exp(scores - highest)
        probabilities = (expo / lax.optimization_barrier(jnp.sum(expo, axis=1, keepdims=True))).astype(jnp.bfloat16)
        contribution = jnp.dot(probabilities.T, grad_block, preferred_element_type=jnp.float32)
        current = lax.dynamic_slice_in_dim(totals, offset, window, 0)
        totals = lax.dynamic_update_slice_in_dim(totals, current + contribution, offset, 0)
        return (totals, None)
    initial = jnp.zeros((length + reach, head_width), jnp.float32)
    totals, _ = lax.scan(one_block, initial, jnp.arange(length // query_rows, dtype=jnp.int32))
    return totals[reach:].astype(jnp.bfloat16)

def block_segment(blocks_row, amount):
    ends = jnp.cumsum(blocks_row)
    return lax.optimization_barrier(jnp.sum((jnp.arange(amount, dtype=jnp.int32)[:, None] >= ends[None, :]).astype(jnp.int32), axis=1))

def reference(normed_hidden_input, frozen_query_rows, frozen_key_rows, attention_output_gradient, adapter_down_weight, adapter_up_weight, segment_adapter_index, segment_block_count, adapter_row_index):
    block_total = SEQLEN // BLOCK
    reach = MOSTBLK * BLOCK
    group_size = HEADS // KV_HEADS

    def one_sequence(running, number):
        down_totals, up_totals = running
        offset = number * SEQLEN
        seq_hidden = lax.dynamic_slice_in_dim(normed_hidden_input, offset, SEQLEN, 0)
        seq_queries = lax.dynamic_slice_in_dim(frozen_query_rows, offset, SEQLEN, 0)
        seq_keys = lax.dynamic_slice_in_dim(frozen_key_rows, offset, SEQLEN, 0)
        seq_grads = lax.dynamic_slice_in_dim(attention_output_gradient, offset, SEQLEN, 0)
        segment_of_block = block_segment(segment_block_count[number], block_total)
        tenant_of_block = segment_adapter_index[number][segment_of_block]
        block_slot_index = adapter_row_index[tenant_of_block].astype(jnp.int32)
        segment_ids = jnp.broadcast_to(segment_of_block[:, None], (block_total, BLOCK)).reshape(SEQLEN)
        down_weight_blocks = adapter_down_weight[block_slot_index]
        up_weight_blocks = adapter_up_weight[block_slot_index]
        hidden_input_blocks = seq_hidden.reshape(block_total, BLOCK, MODEL_WIDTH)
        reduced_rank_part = jnp.einsum('jyw,jaw->jya', hidden_input_blocks.astype(jnp.float32), down_weight_blocks.astype(jnp.float32)).astype(jnp.bfloat16)
        query_heads = jnp.transpose(seq_queries.reshape(SEQLEN, HEADS, HEAD_DIM), (1, 0, 2))
        key_heads = jnp.transpose(jnp.repeat(seq_keys.reshape(SEQLEN, KV_HEADS, HEAD_DIM), group_size, axis=1), (1, 0, 2))
        grad_heads = jnp.transpose(seq_grads.reshape(SEQLEN, HEADS, HEAD_DIM), (1, 0, 2))

        def per_head(triple):
            return attend_head(triple[0], triple[1], triple[2], segment_ids, QROWS, reach)
        head_grad = lax.map(per_head, (query_heads, key_heads, grad_heads))
        value_grad = lax.optimization_barrier(jnp.sum(head_grad.reshape(KV_HEADS, group_size, SEQLEN, HEAD_DIM), axis=1, dtype=jnp.float32))
        value_grad = jnp.transpose(value_grad, (1, 0, 2)).reshape(SEQLEN, VALUE_WIDTH).astype(jnp.bfloat16)
        value_row_blocks = value_grad.reshape(block_total, BLOCK, VALUE_WIDTH)
        up_weight_terms = adapter_scale * jnp.einsum('fvg,fvn->fgn', reduced_rank_part.astype(jnp.float32), value_row_blocks.astype(jnp.float32))
        backward_rank_part = (adapter_scale * jnp.einsum('vaw,vpw->vap', value_row_blocks.astype(jnp.float32), up_weight_blocks.astype(jnp.float32))).astype(jnp.bfloat16)
        down_weight_terms = jnp.einsum('jcy,jct->jyt', backward_rank_part.astype(jnp.float32), hidden_input_blocks.astype(jnp.float32))
        down_totals = down_totals.at[block_slot_index].add(down_weight_terms)
        up_totals = up_totals.at[block_slot_index].add(up_weight_terms)
        return ((down_totals, up_totals), None)
    initial = (jnp.zeros((ADAPTER_COUNT, ADAPTER_RANK, MODEL_WIDTH), jnp.float32), jnp.zeros((ADAPTER_COUNT, ADAPTER_RANK, VALUE_WIDTH), jnp.float32))
    (down_totals, up_totals), _ = lax.scan(one_sequence, initial, jnp.arange(N_GRP, dtype=jnp.int32))
    return (down_totals, up_totals)
```

```python
import functools
import math

import jax
import jax.numpy as jnp
from jax import lax
from jax.experimental import pallas as pl
from jax.experimental.pallas import tpu as pltpu
from jax.sharding import PartitionSpec as P

HEAD_DIM = 128
BLOCK = 128
LONG = 16
CAP = 2
ROWS = 80
NEG = -1e30
FACTOR = 1.0 / math.sqrt(HEAD_DIM)

COLUMN = [[8 * x + 2 * q + p for x in range(4) for p in range(2)] for q in range(4)]
ROW = [[8 * x + 2 * q + p for q in range(4)] for x in range(4) for p in range(2)]

VMEM = pl.BlockSpec(memory_space=pltpu.VMEM)
ANY = pl.BlockSpec(memory_space=pl.ANY)
F32 = jnp.float32
BF16 = jnp.bfloat16


def dot_nt(a, b):
    return lax.dot_general(a, b, (((1,), (1,)), ((), ())), preferred_element_type=F32)


def dot_tn(a, b):
    return lax.dot_general(a, b, (((0,), (0,)), ((), ())), preferred_element_type=F32)


def dot_nn(a, b):
    return jnp.dot(a, b, preferred_element_type=F32)


def stack_heads(rows):
    return jnp.concatenate([rows[:, h * 128 : (h + 1) * 128] for h in range(4)], axis=0)


def pack_kernel(q_ref, g_ref, k_ref, out_ref):
    for h in range(8):
        out_ref[h, :, :512] = q_ref[:, 512 * h : 512 * (h + 1)]
        out_ref[h, :, 512:1024] = g_ref[:, 512 * h : 512 * (h + 1)]
        out_ref[h, :, 1024:] = k_ref[:, 128 * h : 128 * (h + 1)]


def pack(q, g, k):
    return pl.pallas_call(
        pack_kernel,
        name="pack",
        out_shape=jax.ShapeDtypeStruct((8, 128, 1152), BF16),
        grid=(4,),
        in_specs=[
            pl.BlockSpec((32, 4096), lambda i: (i, 0)),
            pl.BlockSpec((32, 4096), lambda i: (i, 0)),
            pl.BlockSpec((32, 1024), lambda i: (i, 0)),
        ],
        out_specs=pl.BlockSpec((8, 32, 1152), lambda i: (0, i, 0)),
        cost_estimate=pl.CostEstimate(flops=0, bytes_accessed=5 << 20, transcendentals=0),
    )(q, g, k)


def pick_kernel(slot_ref, all_ref, out_ref, sems):
    started = [
        pltpu.make_async_copy(all_ref.at[slot_ref[b]], out_ref.at[b], sems.at[b]) for b in range(32)
    ]
    for c in started:
        c.start()
    for c in started:
        c.wait()


def pick(slots, gathered):
    return pl.pallas_call(
        pick_kernel,
        name="pick",
        out_shape=jax.ShapeDtypeStruct((32, ROWS, 128), BF16),
        in_specs=[pl.BlockSpec(memory_space=pltpu.SMEM), ANY],
        out_specs=VMEM,
        scratch_shapes=[pltpu.SemaphoreType.DMA((32,))],
        cost_estimate=pl.CostEstimate(flops=0, bytes_accessed=1 << 20, transcendentals=0),
    )(slots, gathered)


def long_kernel(tab_ref, recv_ref, key_ref, out_ref, keys, acc, sc):
    i = pl.program_id(0)

    @pl.when(i == 0)
    def _():
        acc[...] = jnp.zeros_like(acc)
        for j in range(LONG):
            keys[pl.ds(128 * j, 128), :] = key_ref[tab_ref[8 + j]]

    own = recv_ref[0]
    queries = stack_heads(own[:, :512])
    grads = stack_heads(own[:, 512:1024])
    pos = tab_ref[4 + i]
    last = pos // 2

    def scores(c):
        start = pl.multiple_of(c * 256, 256)
        return dot_nt(keys[pl.ds(start, 256), :], queries) * FACTOR

    def fold(s):
        return jnp.max(s.reshape(32, 8, 512), axis=0)

    def first(c, top):
        s = scores(c)
        sc[c] = s
        return jnp.maximum(top, fold(s))

    s = scores(last)
    key_at = lax.broadcasted_iota(jnp.int32, (256, 512), 0) + last * 256
    query_at = (lax.broadcasted_iota(jnp.int32, (256, 512), 1) & 127) + pos * 128
    s = jnp.where(key_at <= query_at, s, NEG)
    sc[last] = s
    top = lax.fori_loop(0, last, first, fold(s))
    top = jnp.max(top, axis=0, keepdims=True)

    def second(c, total):
        e = jnp.exp(sc[c] - top)
        sc[c] = e
        return total + jnp.sum(e.reshape(32, 8, 512), axis=0)

    total = lax.fori_loop(0, last + 1, second, jnp.zeros((8, 512), F32))
    inverse = 1.0 / jnp.sum(total, axis=0, keepdims=True)

    def third(c, carry):
        p = (sc[c] * inverse).astype(BF16)
        rows = pl.ds(pl.multiple_of(c * 256, 256), 256)
        acc[rows, :] += dot_nn(p, grads)
        return carry

    lax.fori_loop(0, last + 1, third, 0)

    @pl.when(i == 3)
    def _():
        for j in range(LONG):
            out_ref[tab_ref[24 + j]] = acc[pl.ds(128 * j, 128), :].astype(BF16)


def long_attention(table, recv, keys):
    return pl.pallas_call(
        long_kernel,
        name="long",
        out_shape=jax.ShapeDtypeStruct((LONG, 128, 128), BF16),
        grid_spec=pltpu.PrefetchScalarGridSpec(
            num_scalar_prefetch=1,
            grid=(4,),
            in_specs=[
                pl.BlockSpec((1, 128, 1152), lambda i, t: (t[i], 0, 0)),
                pl.BlockSpec((LONG, 128, 128), lambda i, t: (0, 0, 0)),
            ],
            out_specs=pl.BlockSpec((LONG, 128, 128), lambda i, t: (0, 0, 0)),
            scratch_shapes=[
                pltpu.VMEM((2048, 128), BF16),
                pltpu.VMEM((2048, 128), F32),
                pltpu.VMEM((8, 256, 512), F32),
            ],
        ),
        compiler_params=pltpu.CompilerParams(vmem_limit_bytes=32 << 20),
        cost_estimate=pl.CostEstimate(
            flops=6 << 30, bytes_accessed=3 << 20, transcendentals=8 << 20
        ),
    )(table, recv, keys)


def short_kernel(tab_ref, q_ref, g_ref, k_ref, left_ref, own_ref, prev_ref):
    queries = stack_heads(q_ref[...])
    key_at = lax.broadcasted_iota(jnp.int32, (128, 512), 0)
    query_at = lax.broadcasted_iota(jnp.int32, (128, 512), 1) & 127
    own = jnp.where(key_at <= query_at, dot_nt(k_ref[...], queries) * FACTOR, NEG)
    joined = tab_ref[0] > 0
    prev = jnp.where(joined, dot_nt(left_ref[...], queries) * FACTOR, NEG)
    top = jnp.maximum(jnp.max(own, axis=0, keepdims=True), jnp.max(prev, axis=0, keepdims=True))
    own = jnp.exp(own - top)
    prev = jnp.exp(prev - top)
    total = jnp.sum(own, axis=0, keepdims=True) + jnp.sum(prev, axis=0, keepdims=True)
    inverse = 1.0 / total
    own = (own * inverse).astype(BF16)
    prev = (prev * inverse).astype(BF16)
    summed = jnp.zeros((128, 128), F32)
    for h in range(4):
        lanes = slice(h * 128, (h + 1) * 128)
        summed += dot_nn(own[:, lanes], g_ref[:, lanes]).astype(BF16).astype(F32)
    own_ref[...] = summed
    prev_ref[...] = dot_nn(prev, stack_heads(g_ref[...])).astype(BF16)


def short_attention(table, q, g, k, left):
    wide = pl.BlockSpec((128, 512), lambda i, t: (0, i))
    thin = pl.BlockSpec((128, 128), lambda i, t: (0, i))
    return pl.pallas_call(
        short_kernel,
        name="short",
        out_shape=(
            jax.ShapeDtypeStruct((128, 1024), F32),
            jax.ShapeDtypeStruct((128, 1024), BF16),
        ),
        grid_spec=pltpu.PrefetchScalarGridSpec(
            num_scalar_prefetch=1,
            grid=(8,),
            in_specs=[wide, wide, thin, thin],
            out_specs=(thin, thin),
        ),
        cost_estimate=pl.CostEstimate(
            flops=3 << 30, bytes_accessed=4 << 20, transcendentals=4 << 20
        ),
    )(table, q, g, k, left)


def interleave(transposed):
    row = lax.broadcasted_iota(jnp.int32, (512, 512), 0)
    col = lax.broadcasted_iota(jnp.int32, (512, 512), 1)
    if transposed:
        row, col = col, row
    return (col == (row & 7) * 64 + (row >> 3)).astype(BF16)


def terms_kernel(tab_ref, x_ref, w_ref, far_ref, own_ref, right_ref, out_ref, down):
    for s in range(32):
        down[:, 128 * s : 128 * (s + 1)] = w_ref[s, :64, :]
    low = dot_nt(x_ref[...], down[...]).astype(BF16)
    up = dot_nn(interleave(True), w_ref[:, 64:, :].reshape(512, 128)).astype(BF16)
    is_long = tab_ref[2] > 0
    is_first = tab_ref[1] > 0
    back = jnp.zeros((128, 64), F32)
    up_terms = []
    for c in range(8):
        lanes = slice(c * 128, (c + 1) * 128)
        near = own_ref[:, lanes] + jnp.where(is_first, right_ref[:, lanes].astype(F32), 0.0)
        value = jnp.where(is_long, far_ref[c].astype(F32), near).astype(BF16)
        back += dot_nt(value, up[64 * c : 64 * (c + 1), :])
        up_terms.append((2.0 * dot_tn(low, value)).astype(BF16))
    mixed = dot_nn(interleave(False), jnp.concatenate(up_terms, axis=0)).astype(BF16)
    out_ref[:, 64:, :] = mixed.reshape(32, 16, 128)
    back = (2.0 * back).astype(BF16)
    for s in range(32):
        out_ref[s, :64, :] = dot_tn(back, x_ref[:, 128 * s : 128 * (s + 1)]).astype(BF16)


def terms(table, x, weights, far, own, right):
    return pl.pallas_call(
        terms_kernel,
        name="terms",
        out_shape=jax.ShapeDtypeStruct((32, ROWS, 128), BF16),
        in_specs=[pl.BlockSpec(memory_space=pltpu.SMEM)] + [VMEM] * 5,
        out_specs=VMEM,
        scratch_shapes=[pltpu.VMEM((64, 4096), BF16)],
        compiler_params=pltpu.CompilerParams(vmem_limit_bytes=32 << 20),
        cost_estimate=pl.CostEstimate(flops=1 << 30, bytes_accessed=4 << 20, transcendentals=0),
    )(table, x, weights, far, own, right)


def gather_sum(tab_ref, in_ref, acc):
    acc[...] = jnp.zeros_like(acc)
    for b in range(32):
        acc[tab_ref[b]] += in_ref[b].astype(F32)


def segment_kernel(tab_ref, in_ref, out_ref, acc):
    gather_sum(tab_ref, in_ref, acc)
    out_ref[...] = acc[...].astype(BF16)


def segment_sum(table, parts):
    return pl.pallas_call(
        segment_kernel,
        name="segments",
        out_shape=jax.ShapeDtypeStruct((32, ROWS, 128), BF16),
        in_specs=[pl.BlockSpec(memory_space=pltpu.SMEM), VMEM],
        out_specs=VMEM,
        scratch_shapes=[pltpu.VMEM((32, ROWS, 128), F32)],
    )(table, parts)


def adapter_kernel(tab_ref, in_ref, down_ref, up_ref, acc):
    gather_sum(tab_ref, in_ref, acc)
    down_ref[...] = acc[:16, :64, :]
    for r in range(2):
        for c in range(8):
            up_ref[:, r, 128 * c : 128 * (c + 1)] = acc[:16, 64 + 8 * r + c, :]


def adapter_sum(table, parts):
    return pl.pallas_call(
        adapter_kernel,
        name="adapters",
        out_shape=(
            jax.ShapeDtypeStruct((16, 64, 128), F32),
            jax.ShapeDtypeStruct((16, 2, 1024), F32),
        ),
        in_specs=[pl.BlockSpec(memory_space=pltpu.SMEM), VMEM],
        out_specs=(VMEM, VMEM),
        scratch_shapes=[pltpu.VMEM((24, ROWS, 128), F32)],
    )(table, parts)


def exchange(value, axis, groups=None):
    return lax.all_to_all(value, axis, 0, 0, axis_index_groups=groups, tiled=True)


def row_shift(value, step):
    pairs = [
        (8 * x + 2 * q + p, 8 * x + 2 * ((q + step) % 4) + p)
        for x in range(4)
        for q in range(4)
        for p in range(2)
    ]
    return lax.ppermute(value, "seq", pairs)


def rows_gather(value, y2):
    return jnp.concatenate([value] + [row_shift(value, n) for n in (1, 2, 3)], axis=0)


def rows_sum(value, y2):
    total = lax.dynamic_index_in_dim(value, y2, 0, keepdims=False).astype(F32)
    for n in (1, 2, 3):
        piece = lax.dynamic_index_in_dim(value, (y2 + n) % 4, 0, keepdims=False)
        total += row_shift(piece, n).astype(F32)
    return total.astype(BF16)


def local(x, q, k, g, down_weight, up_weight, seg_adapter, seg_blocks, row_index):
    group = lax.axis_index("grp")
    place = lax.axis_index("seq")
    residents = down_weight.shape[0]
    i32 = jnp.int32

    own_weights = jnp.concatenate([down_weight, up_weight.reshape(residents, 16, 128)], axis=1)
    gathered = lax.all_gather(own_weights, "grp", axis=0, tiled=True)

    sent = pack(q, g, k)
    received = exchange(sent, "seq", COLUMN)

    ids = jnp.arange(row_index.shape[0], dtype=i32)
    slot_of = jnp.sum(jnp.where(seg_adapter[:, :, None] == ids, row_index, 0), axis=2)
    owner = slot_of // residents
    inner = slot_of % residents
    order = jnp.arange(16, dtype=i32)
    earlier = order[:, None] > order[None, :]
    rank = jnp.sum(((owner[:, :, None] == owner[:, None, :]) & earlier).astype(i32), axis=2)
    mine = owner == group
    target = jnp.stack(
        [jnp.min(jnp.where(mine & (rank == c), inner, 16), axis=1) for c in range(CAP)], axis=1
    ).reshape(32)

    counts = lax.dynamic_index_in_dim(seg_blocks, group, 0, keepdims=False)
    ends = jnp.sum(jnp.where(order[:, None] >= order[None, :], counts[None, :], 0), axis=1)
    starts = ends - counts
    blocks = jnp.arange(32, dtype=i32)
    inside = (blocks[:, None] >= starts[None, :]) & (blocks[:, None] < ends[None, :])
    own_slots = lax.dynamic_index_in_dim(slot_of, group, 0, keepdims=False)
    own_places = lax.dynamic_index_in_dim(owner * CAP + rank, group, 0, keepdims=False)
    block_slot = jnp.sum(jnp.where(inside, own_slots[None, :], 0), axis=1)
    block_place = jnp.sum(jnp.where(inside, own_places[None, :], 0), axis=1)
    long_start = jnp.sum(jnp.where(counts == LONG, starts, 0))
    pair_start = jnp.sum(jnp.where(counts == 2, starts, 0))
    flags = jnp.stack(
        [
            place == pair_start + 1,
            place == pair_start,
            (place >= long_start) & (place < long_start + LONG),
        ]
    ).astype(i32)

    y2 = (place % 8) // 2
    four = jnp.arange(4, dtype=i32)
    residue = 8 * (four // 2) + 2 * y2 + four % 2
    high = (residue < long_start).astype(i32)
    source = four + 4 * high
    sixteen = (long_start + order) % 16
    within = sixteen // 8 * 2 + sixteen % 2
    home = (sixteen % 8) // 2
    table = jnp.concatenate(
        [source, (residue - long_start) % 16, (y2 - home) % 4 * 4 + within, home * 4 + within]
    )

    halves = received.reshape(2, 4, 128, 1152)[:, :, :, 1024:]
    long_keys = jnp.where(high[:, None, None] > 0, halves[1], halves[0])
    keys = rows_gather(long_keys, y2)

    picked, keys = lax.optimization_barrier((pick(block_slot, gathered), keys))
    weights = exchange(picked, "seq")
    left = lax.ppermute(k, "seq", [(b, b + 1) for b in range(31)])
    own_value, prev_value = short_attention(flags, q, g, k, left)
    right = lax.ppermute(prev_value, "seq", [(b + 1, b) for b in range(31)])

    partial = long_attention(table, received, keys)
    partial, weights, own_value, right = lax.optimization_barrier(
        (partial, weights, own_value, right)
    )
    head_value = rows_sum(partial.reshape(4, 4, 128, 128), y2)
    far = exchange(jnp.concatenate([head_value, head_value], axis=0), "seq", COLUMN)

    parts = exchange(terms(flags, x, weights, far, own_value, right), "seq")
    sums = exchange(segment_sum(block_place, parts), "grp")
    return adapter_sum(target, sums)


def solution(mesh):
    rows = P(("grp", "seq"), None)
    return jax.shard_map(
        local,
        mesh=mesh,
        in_specs=(rows,) * 4 + (P("grp", None, "seq"), P("grp", "seq", None)) + (P(),) * 3,
        out_specs=(P("grp", None, "seq"), P("grp", "seq", None)),
        check_vma=False,
    )
```

```python
import math

import jax
import jax.numpy as jnp
from jax import lax
from jax.experimental import pallas as pl
from jax.experimental.pallas import tpu as pltpu
from jax.sharding import PartitionSpec as P

HEAD_DIM = 128
BLOCK = 128
LONG = 16
CAP = 2
ROWS = 80
NEG = -1e30
FACTOR = 1.0 / math.sqrt(HEAD_DIM)

COLUMN = [[8 * x + 2 * q + p for x in range(4) for p in range(2)] for q in range(4)]

VMEM = pl.BlockSpec(memory_space=pltpu.VMEM)
SMEM = pl.BlockSpec(memory_space=pltpu.SMEM)
F32 = jnp.float32
BF16 = jnp.bfloat16


def dot_nt(a, b):
    return lax.dot_general(a, b, (((1,), (1,)), ((), ())), preferred_element_type=F32)


def dot_tn(a, b):
    return lax.dot_general(a, b, (((0,), (0,)), ((), ())), preferred_element_type=F32)


def dot_nn(a, b):
    return jnp.dot(a, b, preferred_element_type=F32)


def stack_heads(rows):
    return jnp.concatenate([rows[:, h * 128 : (h + 1) * 128] for h in range(4)], axis=0)


def pack_kernel(q_ref, g_ref, k_ref, out_ref):
    for h in range(8):
        out_ref[h, :, :512] = q_ref[:, 512 * h : 512 * (h + 1)]
        out_ref[h, :, 512:1024] = g_ref[:, 512 * h : 512 * (h + 1)]
        out_ref[h, :, 1024:] = k_ref[:, 128 * h : 128 * (h + 1)]


def pack(q, g, k):
    def rows(width):
        return pl.BlockSpec((32, width), lambda i: (i, 0))

    return pl.pallas_call(
        pack_kernel,
        name="pack",
        out_shape=jax.ShapeDtypeStruct((8, 128, 1152), BF16),
        grid=(4,),
        in_specs=[rows(4096), rows(4096), rows(1024)],
        out_specs=pl.BlockSpec((8, 32, 1152), lambda i: (0, i, 0)),
        cost_estimate=pl.CostEstimate(flops=0, bytes_accessed=5 << 20, transcendentals=0),
    )(q, g, k)


def choose_kernel(tab_ref, down_ref, up_ref, out_ref):
    for n in range(32):
        row = jnp.minimum(tab_ref[n], 15)
        out_ref[n, :64, :] = down_ref[row]
        out_ref[n, 64:, :] = up_ref[row]


def choose(table, down, up):
    return pl.pallas_call(
        choose_kernel,
        name="choose",
        out_shape=jax.ShapeDtypeStruct((32, ROWS, 128), BF16),
        in_specs=[SMEM, VMEM, VMEM],
        out_specs=VMEM,
        cost_estimate=pl.CostEstimate(flops=0, bytes_accessed=1 << 20, transcendentals=0),
    )(table, down, up)


def pick_kernel(tab_ref, in_ref, out_ref):
    for b in range(32):
        out_ref[b] = in_ref[tab_ref[b]]


def pick(table, fetched):
    return pl.pallas_call(
        pick_kernel,
        name="pick",
        out_shape=jax.ShapeDtypeStruct((32, ROWS, 128), BF16),
        in_specs=[SMEM, VMEM],
        out_specs=VMEM,
        cost_estimate=pl.CostEstimate(flops=0, bytes_accessed=1 << 20, transcendentals=0),
    )(table, fetched)


def long_kernel(tab_ref, own_ref, key_ref, out_ref, keys, acc, sc):
    i = pl.program_id(0)

    @pl.when(i == 0)
    def _():
        acc[...] = jnp.zeros_like(acc)
        for j in range(LONG + 1):
            keys[pl.ds(128 * j, 128), :] = key_ref[tab_ref[10 + j]]

    pos = tab_ref[5 + i]
    last = pos // 2
    base = jnp.where(i == 4, LONG * 128, 0)

    @pl.when(pos >= 0)
    def _():
        own = own_ref[0]
        queries = stack_heads(own[:, :512])
        grads = stack_heads(own[:, 512:1024])

        @pl.when(i == 4)
        def _():
            keys[pl.ds(2176, 128), :] = own[:, 1024:]

        def rows(c):
            return pl.ds(pl.multiple_of(base + c * 256, 256), 256)

        def scores(c):
            return dot_nt(keys[rows(c), :], queries) * FACTOR

        def fold(s):
            return jnp.max(s.reshape(32, 8, 512), axis=0)

        def first(c, top):
            s = scores(c)
            sc[c] = s
            return jnp.maximum(top, fold(s))

        s = scores(last)
        key_at = lax.broadcasted_iota(jnp.int32, (256, 512), 0) + last * 256
        query_at = (lax.broadcasted_iota(jnp.int32, (256, 512), 1) & 127) + pos * 128
        s = jnp.where(key_at <= query_at, s, NEG)
        sc[last] = s
        top = lax.fori_loop(0, last, first, fold(s))
        top = jnp.max(top, axis=0, keepdims=True)

        def second(c, total):
            e = jnp.exp(sc[c] - top)
            sc[c] = e
            return total + jnp.sum(e.reshape(32, 8, 512), axis=0)

        total = lax.fori_loop(0, last + 1, second, jnp.zeros((8, 512), F32))
        inverse = 1.0 / jnp.sum(total, axis=0, keepdims=True)

        def third(c, carry):
            p = (sc[c] * inverse).astype(BF16)
            acc[rows(c), :] += dot_nn(p, grads)
            return carry

        lax.fori_loop(0, last + 1, third, 0)

    @pl.when(i == 4)
    def _():
        for j in range(LONG):
            out_ref[tab_ref[27 + j]] = acc[pl.ds(128 * j, 128), :].astype(BF16)
        shared = acc[2048:2176, :].astype(BF16)
        out_ref[4] = shared
        out_ref[17] = shared
        out_ref[18] = acc[2176:, :].astype(BF16)


def long_attention(table, received, keys):
    def whole(*shape):
        return pl.BlockSpec(shape, lambda i, t: (0,) * len(shape))

    return pl.pallas_call(
        long_kernel,
        name="long",
        out_shape=jax.ShapeDtypeStruct((19, 128, 128), BF16),
        grid_spec=pltpu.PrefetchScalarGridSpec(
            num_scalar_prefetch=1,
            grid=(5,),
            in_specs=[
                pl.BlockSpec((1, 128, 1152), lambda i, t: (t[i], 0, 0)),
                whole(18, 128, 128),
            ],
            out_specs=whole(19, 128, 128),
            scratch_shapes=[
                pltpu.VMEM((2304, 128), BF16),
                pltpu.VMEM((2304, 128), F32),
                pltpu.VMEM((8, 256, 512), F32),
            ],
        ),
        compiler_params=pltpu.CompilerParams(vmem_limit_bytes=32 << 20),
        cost_estimate=pl.CostEstimate(
            flops=6 << 30, bytes_accessed=4 << 20, transcendentals=8 << 20
        ),
    )(table, received, keys)


def short_kernel(q_ref, g_ref, k_ref, out_ref):
    key_at = lax.broadcasted_iota(jnp.int32, (128, 512), 0)
    query_at = lax.broadcasted_iota(jnp.int32, (128, 512), 1) & 127
    s = dot_nt(k_ref[...], stack_heads(q_ref[...])) * FACTOR
    s = jnp.where(key_at <= query_at, s, NEG)
    e = jnp.exp(s - jnp.max(s, axis=0, keepdims=True))
    p = (e * (1.0 / jnp.sum(e, axis=0, keepdims=True))).astype(BF16)
    summed = jnp.zeros((128, 128), F32)
    for h in range(4):
        lanes = slice(h * 128, (h + 1) * 128)
        summed += dot_nn(p[:, lanes], g_ref[:, lanes]).astype(BF16).astype(F32)
    out_ref[...] = summed.astype(BF16)


def short_attention(q, g, k):
    wide = pl.BlockSpec((128, 512), lambda i: (0, i))
    thin = pl.BlockSpec((128, 128), lambda i: (0, i))
    return pl.pallas_call(
        short_kernel,
        name="short",
        out_shape=jax.ShapeDtypeStruct((128, 1024), BF16),
        grid=(8,),
        in_specs=[wide, wide, thin],
        out_specs=thin,
        cost_estimate=pl.CostEstimate(
            flops=3 << 30, bytes_accessed=4 << 20, transcendentals=4 << 20
        ),
    )(q, g, k)


def interleave(transposed):
    row = lax.broadcasted_iota(jnp.int32, (512, 512), 0)
    col = lax.broadcasted_iota(jnp.int32, (512, 512), 1)
    if transposed:
        row, col = col, row
    return (col == (row & 7) * 64 + (row >> 3)).astype(BF16)


def terms_kernel(tab_ref, x_ref, w_ref, far_ref, own_ref, out_ref, down):
    for s in range(32):
        down[:, 128 * s : 128 * (s + 1)] = w_ref[s, :64, :]
    low = dot_nt(x_ref[...], down[...]).astype(BF16)
    up = dot_nn(interleave(True), w_ref[:, 64:, :].reshape(512, 128)).astype(BF16)
    near, wide = tab_ref[0] > 0, tab_ref[1] > 0
    back = jnp.zeros((128, 64), F32)
    up_terms = []
    for c in range(8):
        lanes = slice(c * 128, (c + 1) * 128)
        value = jnp.where(near, own_ref[:, lanes].astype(F32), 0.0)
        value = (value + jnp.where(wide, far_ref[c].astype(F32), 0.0)).astype(BF16)
        back += dot_nt(value, up[64 * c : 64 * (c + 1), :])
        up_terms.append((2.0 * dot_tn(low, value)).astype(BF16))
    mixed = dot_nn(interleave(False), jnp.concatenate(up_terms, axis=0)).astype(BF16)
    out_ref[:, 64:, :] = mixed.reshape(32, 16, 128)
    back = (2.0 * back).astype(BF16)
    for s in range(32):
        out_ref[s, :64, :] = dot_tn(back, x_ref[:, 128 * s : 128 * (s + 1)]).astype(BF16)


def terms(table, x, weights, far, own):
    return pl.pallas_call(
        terms_kernel,
        name="terms",
        out_shape=jax.ShapeDtypeStruct((32, ROWS, 128), BF16),
        in_specs=[SMEM] + [VMEM] * 4,
        out_specs=VMEM,
        scratch_shapes=[pltpu.VMEM((64, 4096), BF16)],
        compiler_params=pltpu.CompilerParams(vmem_limit_bytes=32 << 20),
        cost_estimate=pl.CostEstimate(flops=1 << 30, bytes_accessed=4 << 20, transcendentals=0),
    )(table, x, weights, far, own)


def gather_sum(tab_ref, in_ref, acc):
    acc[...] = jnp.zeros_like(acc)
    for b in range(32):
        acc[tab_ref[b]] += in_ref[b].astype(F32)


def segment_kernel(tab_ref, in_ref, out_ref, acc):
    gather_sum(tab_ref, in_ref, acc)
    out_ref[...] = acc[...].astype(BF16)


def segment_sum(table, parts):
    return pl.pallas_call(
        segment_kernel,
        name="segments",
        out_shape=jax.ShapeDtypeStruct((32, ROWS, 128), BF16),
        in_specs=[SMEM, VMEM],
        out_specs=VMEM,
        scratch_shapes=[pltpu.VMEM((32, ROWS, 128), F32)],
    )(table, parts)


def adapter_kernel(tab_ref, in_ref, down_ref, up_ref, acc):
    gather_sum(tab_ref, in_ref, acc)
    down_ref[...] = acc[:16, :64, :]
    for r in range(2):
        for c in range(8):
            up_ref[:, r, 128 * c : 128 * (c + 1)] = acc[:16, 64 + 8 * r + c, :]


def adapter_sum(table, parts):
    return pl.pallas_call(
        adapter_kernel,
        name="adapters",
        out_shape=(
            jax.ShapeDtypeStruct((16, 64, 128), F32),
            jax.ShapeDtypeStruct((16, 2, 1024), F32),
        ),
        in_specs=[SMEM, VMEM],
        out_specs=(VMEM, VMEM),
        scratch_shapes=[pltpu.VMEM((24, ROWS, 128), F32)],
    )(table, parts)


def exchange(value, axis, groups=None):
    return lax.all_to_all(value, axis, 0, 0, axis_index_groups=groups, tiled=True)


def row_shift(value, step):
    pairs = [
        (8 * x + 2 * q + p, 8 * x + 2 * ((q + step) % 4) + p)
        for x in range(4)
        for q in range(4)
        for p in range(2)
    ]
    return lax.ppermute(value, "seq", pairs)


def local(x, q, k, g, down_weight, up_weight, seg_adapter, seg_blocks, row_index):
    group = lax.axis_index("grp")
    place = lax.axis_index("seq")
    residents = down_weight.shape[0]
    i32 = jnp.int32

    received = exchange(pack(q, g, k), "seq", COLUMN)
    own_value = short_attention(q, g, k)

    ids = jnp.arange(row_index.shape[0], dtype=i32)
    slot_of = jnp.sum(jnp.where(seg_adapter[:, :, None] == ids, row_index, 0), axis=2)
    owner = slot_of // residents
    inner = slot_of % residents
    order = jnp.arange(16, dtype=i32)
    earlier = order[:, None] > order[None, :]
    rank = jnp.sum(((owner[:, :, None] == owner[:, None, :]) & earlier).astype(i32), axis=2)
    mine = owner == group
    target = jnp.stack(
        [jnp.min(jnp.where(mine & (rank == c), inner, 16), axis=1) for c in range(CAP)], axis=1
    ).reshape(32)

    counts = lax.dynamic_index_in_dim(seg_blocks, group, 0, keepdims=False)
    ends = jnp.sum(jnp.where(order[:, None] >= order[None, :], counts[None, :], 0), axis=1)
    starts = ends - counts
    blocks = jnp.arange(32, dtype=i32)
    inside = (blocks[:, None] >= starts[None, :]) & (blocks[:, None] < ends[None, :])
    own_places = lax.dynamic_index_in_dim(owner * CAP + rank, group, 0, keepdims=False)
    block_place = jnp.sum(jnp.where(inside, own_places[None, :], 0), axis=1)
    long_start = jnp.sum(jnp.where(counts == LONG, starts, 0))
    pair_start = jnp.sum(jnp.where(counts == 2, starts, 0))
    counted = jnp.sum(jnp.where(inside, counts[None, :], 0), axis=1)
    counted = lax.dynamic_index_in_dim(counted, place, 0)
    flags = jnp.concatenate([(counted == 1) | (place == pair_start), counted > 1]).astype(i32)

    y2 = (place % 8) // 2
    four = jnp.arange(4, dtype=i32)
    residue = 8 * (four // 2) + 2 * y2 + four % 2
    source = jnp.where(residue < long_start, four + 4, four)
    pair = pair_start + jnp.arange(2, dtype=i32)
    pair_member = pair // 8 * 2 + pair % 2
    pair_row = (pair % 8) // 2
    sixteen = (long_start + order) % 16
    within = sixteen // 8 * 2 + sixteen % 2
    home = (sixteen % 8) // 2
    down_row = (y2 - home) % 4
    up_row = (home - y2) % 4
    table = jnp.concatenate(
        [
            source,
            pair_member[1:],
            (residue - long_start) % 16,
            jnp.where(pair_row[1:] == y2, 1, -1),
            jnp.where(down_row == 3, 14, 5 * down_row) + within,
            (y2 - pair_row[:1]) % 2 * 5 + 4,
            4 * up_row + (up_row > 0) + within,
        ]
    )
    members = jnp.arange(8, dtype=i32)[:, None, None]
    is_long = jnp.tile(source, 2)[:, None, None] == members
    is_first = (pair_member[0] == members) & (pair_row[0] == y2)

    halves = received.reshape(2, 4, 128, 1152)[:, :, :, 1024:]
    long_keys = jnp.where((source > 3)[:, None, None], halves[1], halves[0])
    pair_key = lax.dynamic_slice(received, (pair_member[0], 0, 1024), (1, 128, 128))
    long_keys = jnp.concatenate([long_keys, pair_key], axis=0)

    chosen = choose(target, down_weight, up_weight.reshape(residents, 16, 128))
    chosen, long_keys, own_value = lax.optimization_barrier((chosen, long_keys, own_value))
    fetched = exchange(chosen, "grp")
    keys = jnp.concatenate(
        [
            long_keys,
            row_shift(long_keys, 1),
            row_shift(long_keys[:4], 2),
            row_shift(long_keys[:4], 3),
        ],
        axis=0,
    )
    partial = long_attention(table, received, keys)

    picked, _ = lax.optimization_barrier((pick(block_place, fetched), partial))
    weights = exchange(picked, "seq")
    last = row_shift(partial[13:18], 3)
    head_value = (
        partial[:4].astype(F32)
        + row_shift(partial[5:9], 1).astype(F32)
        + row_shift(partial[9:13], 2).astype(F32)
        + last[:4].astype(F32)
    ).astype(BF16)
    first_value = partial[4] + last[4]
    head_value = jnp.where(
        is_long,
        jnp.concatenate([head_value, head_value], axis=0),
        jnp.where(is_first, first_value, partial[18]),
    )
    head_value, weights = lax.optimization_barrier((head_value, weights))
    far = exchange(head_value, "seq", COLUMN)

    parts = exchange(terms(flags, x, weights, far, own_value), "seq")
    sums = exchange(segment_sum(block_place, parts), "grp")
    return adapter_sum(target, sums)


def solution(mesh):
    rows = P(("grp", "seq"), None)
    return jax.shard_map(
        local,
        mesh=mesh,
        in_specs=(rows,) * 4 + (P("grp", None, "seq"), P("grp", "seq", None)) + (P(),) * 3,
        out_specs=(P("grp", None, "seq"), P("grp", "seq", None)),
        check_vma=False,
    )
```

```python
import math

import jax
import jax.numpy as jnp
from jax import lax
from jax.experimental import pallas as pl
from jax.experimental.pallas import tpu as pltpu
from jax.sharding import PartitionSpec as P

HEAD_DIM = 128
BLOCK = 128
LONG = 16
CAP = 2
ROWS = 80
NEG = -1e30
FACTOR = math.log2(math.e) / math.sqrt(HEAD_DIM)

ROW = [[8 * x + 2 * q + p for q in range(4)] for x in range(4) for p in range(2)]
COLUMN = [[8 * x + 2 * q + p for x in range(4) for p in range(2)] for q in range(4)]

VMEM = pl.BlockSpec(memory_space=pltpu.VMEM)
SMEM = pl.BlockSpec(memory_space=pltpu.SMEM)
F32 = jnp.float32
BF16 = jnp.bfloat16


def dot_nt(a, b):
    return lax.dot_general(a, b, (((1,), (1,)), ((), ())), preferred_element_type=F32)


def dot_tn(a, b):
    return lax.dot_general(a, b, (((0,), (0,)), ((), ())), preferred_element_type=F32)


def dot_nn(a, b):
    return jnp.dot(a, b, preferred_element_type=F32)


def stack_heads(rows):
    return jnp.concatenate([rows[:, h * 128 : (h + 1) * 128] for h in range(4)], axis=0)


def pack_kernel(q_ref, g_ref, k_ref, out_ref):
    for h in range(8):
        out_ref[h, :, :512] = q_ref[:, 512 * h : 512 * (h + 1)]
        out_ref[h, :, 512:1024] = g_ref[:, 512 * h : 512 * (h + 1)]
        out_ref[h, :, 1024:] = k_ref[:, 128 * h : 128 * (h + 1)]


def pack(q, g, k):
    def rows(width):
        return pl.BlockSpec((32, width), lambda i: (i, 0))

    return pl.pallas_call(
        pack_kernel,
        name="pack",
        out_shape=jax.ShapeDtypeStruct((8, 128, 1152), BF16),
        grid=(4,),
        in_specs=[rows(4096), rows(4096), rows(1024)],
        out_specs=pl.BlockSpec((8, 32, 1152), lambda i: (0, i, 0)),
        cost_estimate=pl.CostEstimate(flops=0, bytes_accessed=5 << 20, transcendentals=0),
    )(q, g, k)


def choose_kernel(tab_ref, down_ref, up_ref, out_ref):
    for n in range(32):
        row = jnp.minimum(tab_ref[n], 15)
        out_ref[n, :64, :] = down_ref[row]
        out_ref[n, 64:, :] = up_ref[row]


def choose(table, down, up):
    return pl.pallas_call(
        choose_kernel,
        name="choose",
        out_shape=jax.ShapeDtypeStruct((32, ROWS, 128), BF16),
        in_specs=[SMEM, VMEM, VMEM],
        out_specs=VMEM,
        cost_estimate=pl.CostEstimate(flops=0, bytes_accessed=1 << 20, transcendentals=0),
    )(table, down, up)


def pick_kernel(tab_ref, in_ref, out_ref):
    for b in range(32):
        out_ref[b] = in_ref[tab_ref[b]]


def pick(table, fetched):
    return pl.pallas_call(
        pick_kernel,
        name="pick",
        out_shape=jax.ShapeDtypeStruct((32, ROWS, 128), BF16),
        in_specs=[SMEM, VMEM],
        out_specs=VMEM,
        cost_estimate=pl.CostEstimate(flops=0, bytes_accessed=1 << 20, transcendentals=0),
    )(table, fetched)


def long_kernel(tab_ref, own_ref, key_ref, out_ref, keys, acc, sc):
    i = pl.program_id(0)

    @pl.when(i == 0)
    def _():
        acc[...] = jnp.zeros_like(acc)
        for j in range(LONG + 1):
            keys[pl.ds(128 * j, 128), :] = key_ref[tab_ref[10 + j]]

    pos = tab_ref[5 + i]
    last = pos // 2
    base = jnp.where(i == 4, LONG * 128, 0)

    @pl.when(pos >= 0)
    def _():
        own = own_ref[0]
        queries = stack_heads(own[:, :512])
        grads = stack_heads(own[:, 512:1024])

        @pl.when(i == 4)
        def _():
            keys[pl.ds(2176, 128), :] = own[:, 1024:]

        def rows(c):
            return pl.ds(pl.multiple_of(base + c * 256, 256), 256)

        def scores(c):
            return dot_nt(keys[rows(c), :], queries)

        def fold(s):
            return jnp.max(s.reshape(32, 8, 512), axis=0)

        def first(c, top):
            s = scores(c)
            sc[c] = s
            return jnp.maximum(top, fold(s))

        s = scores(last)
        key_at = lax.broadcasted_iota(jnp.int32, (256, 512), 0) + last * 256
        query_at = (lax.broadcasted_iota(jnp.int32, (256, 512), 1) & 127) + pos * 128
        s = jnp.where(key_at <= query_at, s, NEG)
        sc[last] = s
        top = lax.fori_loop(0, last, first, fold(s))
        top = jnp.max(top, axis=0, keepdims=True)

        def second(c, total):
            e = jnp.exp2((sc[c] - top) * FACTOR)
            sc[c] = e
            return total + jnp.sum(e.reshape(32, 8, 512), axis=0)

        total = lax.fori_loop(0, last + 1, second, jnp.zeros((8, 512), F32))
        inverse = 1.0 / jnp.sum(total, axis=0, keepdims=True)

        def third(c, carry):
            p = (sc[c] * inverse).astype(BF16)
            acc[rows(c), :] += dot_nn(p, grads)
            return carry

        lax.fori_loop(0, last + 1, third, 0)

    @pl.when(i == 4)
    def _():
        for j in range(LONG):
            out_ref[tab_ref[27 + j]] = acc[pl.ds(128 * j, 128), :].astype(BF16)
        shared = acc[2048:2176, :].astype(BF16)
        out_ref[4] = shared
        out_ref[17] = shared
        out_ref[18] = acc[2176:, :].astype(BF16)


def long_attention(table, received, keys):
    def whole(*shape):
        return pl.BlockSpec(shape, lambda i, t: (0,) * len(shape))

    return pl.pallas_call(
        long_kernel,
        name="long",
        out_shape=jax.ShapeDtypeStruct((19, 128, 128), BF16),
        grid_spec=pltpu.PrefetchScalarGridSpec(
            num_scalar_prefetch=1,
            grid=(5,),
            in_specs=[
                pl.BlockSpec((1, 128, 1152), lambda i, t: (t[i], 0, 0)),
                whole(20, 128, 128),
            ],
            out_specs=whole(19, 128, 128),
            scratch_shapes=[
                pltpu.VMEM((2304, 128), BF16),
                pltpu.VMEM((2304, 128), F32),
                pltpu.VMEM((8, 256, 512), F32),
            ],
        ),
        compiler_params=pltpu.CompilerParams(vmem_limit_bytes=32 << 20),
        cost_estimate=pl.CostEstimate(
            flops=6 << 30, bytes_accessed=4 << 20, transcendentals=8 << 20
        ),
    )(table, received, keys)


def short_kernel(q_ref, g_ref, k_ref, out_ref):
    key_at = lax.broadcasted_iota(jnp.int32, (128, 512), 0)
    query_at = lax.broadcasted_iota(jnp.int32, (128, 512), 1) & 127
    s = dot_nt(k_ref[...], stack_heads(q_ref[...]))
    s = jnp.where(key_at <= query_at, s, NEG)
    e = jnp.exp2((s - jnp.max(s, axis=0, keepdims=True)) * FACTOR)
    p = (e * (1.0 / jnp.sum(e, axis=0, keepdims=True))).astype(BF16)
    summed = jnp.zeros((128, 128), F32)
    for h in range(4):
        lanes = slice(h * 128, (h + 1) * 128)
        summed += dot_nn(p[:, lanes], g_ref[:, lanes]).astype(BF16).astype(F32)
    out_ref[...] = summed.astype(BF16)


def short_attention(q, g, k):
    wide = pl.BlockSpec((128, 512), lambda i: (0, i))
    thin = pl.BlockSpec((128, 128), lambda i: (0, i))
    return pl.pallas_call(
        short_kernel,
        name="short",
        out_shape=jax.ShapeDtypeStruct((128, 1024), BF16),
        grid=(8,),
        in_specs=[wide, wide, thin],
        out_specs=thin,
        cost_estimate=pl.CostEstimate(
            flops=3 << 30, bytes_accessed=4 << 20, transcendentals=4 << 20
        ),
    )(q, g, k)


def interleave(transposed):
    row = lax.broadcasted_iota(jnp.int32, (512, 512), 0)
    col = lax.broadcasted_iota(jnp.int32, (512, 512), 1)
    if transposed:
        row, col = col, row
    return (col == (row & 7) * 64 + (row >> 3)).astype(BF16)


def low_kernel(x_ref, w_ref, low_ref, up_ref, down):
    for s in range(32):
        down[:, 128 * s : 128 * (s + 1)] = w_ref[s, :64, :]
    low_ref[...] = dot_nt(x_ref[...], down[...]).astype(BF16)
    up_ref[...] = dot_nn(interleave(True), w_ref[:, 64:, :].reshape(512, 128)).astype(BF16)


def low_rank(x, weights):
    return pl.pallas_call(
        low_kernel,
        name="low",
        out_shape=(
            jax.ShapeDtypeStruct((128, 64), BF16),
            jax.ShapeDtypeStruct((512, 128), BF16),
        ),
        in_specs=[VMEM] * 2,
        out_specs=(VMEM, VMEM),
        scratch_shapes=[pltpu.VMEM((64, 4096), BF16)],
        cost_estimate=pl.CostEstimate(flops=1 << 28, bytes_accessed=2 << 20, transcendentals=0),
    )(x, weights)


def terms_kernel(tab_ref, x_ref, low_ref, up_ref, far_ref, own_ref, out_ref):
    low = low_ref[...]
    near, wide = tab_ref[0] > 0, tab_ref[1] > 0
    back = jnp.zeros((128, 64), F32)
    up_terms = []
    for c in range(8):
        lanes = slice(c * 128, (c + 1) * 128)
        value = jnp.where(near, own_ref[:, lanes].astype(F32), 0.0)
        value = (value + jnp.where(wide, far_ref[c].astype(F32), 0.0)).astype(BF16)
        back += dot_nt(value, up_ref[64 * c : 64 * (c + 1), :])
        up_terms.append((2.0 * dot_tn(low, value)).astype(BF16))
    back = (2.0 * back).astype(BF16)
    for s in range(32):
        out_ref[s, :64, :] = dot_tn(back, x_ref[:, 128 * s : 128 * (s + 1)]).astype(BF16)
    mixed = dot_nn(interleave(False), jnp.concatenate(up_terms, axis=0)).astype(BF16)
    out_ref[:, 64:, :] = mixed.reshape(32, 16, 128)


def terms(table, x, low, up, far, own):
    return pl.pallas_call(
        terms_kernel,
        name="terms",
        out_shape=jax.ShapeDtypeStruct((32, ROWS, 128), BF16),
        in_specs=[SMEM] + [VMEM] * 5,
        out_specs=VMEM,
        compiler_params=pltpu.CompilerParams(vmem_limit_bytes=32 << 20),
        cost_estimate=pl.CostEstimate(flops=1 << 29, bytes_accessed=4 << 20, transcendentals=0),
    )(table, x, low, up, far, own)


def gather_sum(tab_ref, in_ref, acc):
    acc[...] = jnp.zeros_like(acc)
    for b in range(32):
        acc[tab_ref[b]] += in_ref[b].astype(F32)


def segment_kernel(tab_ref, in_ref, out_ref, acc):
    gather_sum(tab_ref, in_ref, acc)
    out_ref[...] = acc[...].astype(BF16)


def segment_sum(table, parts):
    return pl.pallas_call(
        segment_kernel,
        name="segments",
        out_shape=jax.ShapeDtypeStruct((32, ROWS, 128), BF16),
        in_specs=[SMEM, VMEM],
        out_specs=VMEM,
        scratch_shapes=[pltpu.VMEM((32, ROWS, 128), F32)],
    )(table, parts)


def adapter_kernel(tab_ref, in_ref, down_ref, up_ref, acc):
    gather_sum(tab_ref, in_ref, acc)
    down_ref[...] = acc[:16, :64, :]
    for r in range(2):
        for c in range(8):
            up_ref[:, r, 128 * c : 128 * (c + 1)] = acc[:16, 64 + 8 * r + c, :]


def adapter_sum(table, parts):
    return pl.pallas_call(
        adapter_kernel,
        name="adapters",
        out_shape=(
            jax.ShapeDtypeStruct((16, 64, 128), F32),
            jax.ShapeDtypeStruct((16, 2, 1024), F32),
        ),
        in_specs=[SMEM, VMEM],
        out_specs=(VMEM, VMEM),
        scratch_shapes=[pltpu.VMEM((24, ROWS, 128), F32)],
    )(table, parts)


def exchange(value, axis, groups=None):
    return lax.all_to_all(value, axis, 0, 0, axis_index_groups=groups, tiled=True)


def row_shift(value, step):
    pairs = [
        (8 * x + 2 * q + p, 8 * x + 2 * ((q + step) % 4) + p)
        for x in range(4)
        for q in range(4)
        for p in range(2)
    ]
    return lax.ppermute(value, "seq", pairs)


def local(x, q, k, g, down_weight, up_weight, seg_adapter, seg_blocks, row_index):
    group = lax.axis_index("grp")
    place = lax.axis_index("seq")
    residents = down_weight.shape[0]
    i32 = jnp.int32

    received = exchange(pack(q, g, k), "seq", COLUMN)
    own_value = short_attention(q, g, k)

    ids = jnp.arange(row_index.shape[0], dtype=i32)
    slot_of = jnp.sum(jnp.where(seg_adapter[:, :, None] == ids, row_index, 0), axis=2)
    owner = slot_of // residents
    inner = slot_of % residents
    order = jnp.arange(16, dtype=i32)
    earlier = order[:, None] > order[None, :]
    rank = jnp.sum(((owner[:, :, None] == owner[:, None, :]) & earlier).astype(i32), axis=2)
    mine = owner == group
    target = jnp.stack(
        [jnp.min(jnp.where(mine & (rank == c), inner, 16), axis=1) for c in range(CAP)], axis=1
    ).reshape(32)

    counts = lax.dynamic_index_in_dim(seg_blocks, group, 0, keepdims=False)
    ends = jnp.sum(jnp.where(order[:, None] >= order[None, :], counts[None, :], 0), axis=1)
    starts = ends - counts
    blocks = jnp.arange(32, dtype=i32)
    inside = (blocks[:, None] >= starts[None, :]) & (blocks[:, None] < ends[None, :])
    own_places = lax.dynamic_index_in_dim(owner * CAP + rank, group, 0, keepdims=False)
    block_place = jnp.sum(jnp.where(inside, own_places[None, :], 0), axis=1)
    long_start = jnp.sum(jnp.where(counts == LONG, starts, 0))
    pair_start = jnp.sum(jnp.where(counts == 2, starts, 0))
    counted = jnp.sum(jnp.where(inside, counts[None, :], 0), axis=1)
    counted = lax.dynamic_index_in_dim(counted, place, 0)
    flags = jnp.concatenate([(counted == 1) | (place == pair_start), counted > 1]).astype(i32)

    y2 = (place % 8) // 2
    four = jnp.arange(4, dtype=i32)
    residue = 8 * (four // 2) + 2 * y2 + four % 2
    source = jnp.where(residue < long_start, four + 4, four)
    pair = pair_start + jnp.arange(2, dtype=i32)
    pair_member = pair // 8 * 2 + pair % 2
    pair_row = (pair % 8) // 2
    sixteen = (long_start + order) % 16
    within = sixteen // 8 * 2 + sixteen % 2
    home = (sixteen % 8) // 2
    up_row = (home - y2) % 4
    table = jnp.concatenate(
        [
            source,
            pair_member[1:],
            (residue - long_start) % 16,
            jnp.where(pair_row[1:] == y2, 1, -1),
            5 * home + within,
            5 * pair_row[:1] + 4,
            4 * up_row + (up_row > 0) + within,
        ]
    )
    members = jnp.arange(8, dtype=i32)[:, None, None]
    is_long = jnp.tile(source, 2)[:, None, None] == members
    is_first = (pair_member[0] == members) & (pair_row[0] == y2)

    halves = received.reshape(2, 4, 128, 1152)[:, :, :, 1024:]
    long_keys = jnp.where((source > 3)[:, None, None], halves[1], halves[0])
    pair_key = lax.dynamic_slice(received, (pair_member[0], 0, 1024), (1, 128, 128))
    long_keys = jnp.concatenate([long_keys, pair_key], axis=0)

    chosen = choose(target, down_weight, up_weight.reshape(residents, 16, 128))
    chosen, long_keys, own_value, table, block_place, flags = lax.optimization_barrier(
        (chosen, long_keys, own_value, table, block_place, flags)
    )
    fetched = exchange(chosen, "grp")
    keys = lax.all_gather(long_keys, "seq", axis=0, tiled=True, axis_index_groups=ROW)

    picked, keys = lax.optimization_barrier((pick(block_place, fetched), keys))
    weights = exchange(picked, "seq")
    partial = long_attention(table, received, keys)
    last = row_shift(partial[13:18], 3)
    head_value = (
        partial[:4].astype(F32)
        + row_shift(partial[5:9], 1).astype(F32)
        + row_shift(partial[9:13], 2).astype(F32)
        + last[:4].astype(F32)
    ).astype(BF16)
    first_value = partial[4] + last[4]
    head_value = jnp.where(
        is_long,
        jnp.concatenate([head_value, head_value], axis=0),
        jnp.where(is_first, first_value, partial[18]),
    )
    head_value, weights = lax.optimization_barrier((head_value, weights))
    far = exchange(head_value, "seq", COLUMN)

    parts = exchange(terms(flags, x, *low_rank(x, weights), far, own_value), "seq")
    sums = exchange(segment_sum(block_place, parts), "grp")
    return adapter_sum(target, sums)


def solution(mesh):
    rows = P(("grp", "seq"), None)
    return jax.shard_map(
        local,
        mesh=mesh,
        in_specs=(rows,) * 4 + (P("grp", None, "seq"), P("grp", "seq", None)) + (P(),) * 3,
        out_specs=(P("grp", None, "seq"), P("grp", "seq", None)),
        check_vma=False,
    )
```

```python
import math

import jax
import jax.numpy as jnp
from jax import lax
from jax.experimental import pallas as pl
from jax.experimental.pallas import tpu as pltpu
from jax.sharding import PartitionSpec as P

HEAD_DIM = 128
BLOCK = 128
LONG = 16
CAP = 2
ROWS = 80
NEG = -1e30
FACTOR = math.log2(math.e) / math.sqrt(HEAD_DIM)

ROW = [[8 * x + 2 * q + p for q in range(4)] for x in range(4) for p in range(2)]
COLUMN = [[8 * x + 2 * q + p for x in range(4) for p in range(2)] for q in range(4)]

VMEM = pl.BlockSpec(memory_space=pltpu.VMEM)
SMEM = pl.BlockSpec(memory_space=pltpu.SMEM)
F32 = jnp.float32
BF16 = jnp.bfloat16


def dot_nt(a, b):
    return lax.dot_general(a, b, (((1,), (1,)), ((), ())), preferred_element_type=F32)


def dot_tn(a, b):
    return lax.dot_general(a, b, (((0,), (0,)), ((), ())), preferred_element_type=F32)


def dot_nn(a, b):
    return jnp.dot(a, b, preferred_element_type=F32)


def stack_heads(rows):
    return jnp.concatenate([rows[:, h * 128 : (h + 1) * 128] for h in range(4)], axis=0)


def pack_kernel(q_ref, g_ref, k_ref, out_ref):
    for h in range(8):
        out_ref[h, :, :512] = q_ref[:, 512 * h : 512 * (h + 1)]
        out_ref[h, :, 512:1024] = g_ref[:, 512 * h : 512 * (h + 1)]
        out_ref[h, :, 1024:] = k_ref[:, 128 * h : 128 * (h + 1)]


def pack(q, g, k):
    def rows(width):
        return pl.BlockSpec((32, width), lambda i: (i, 0))

    return pl.pallas_call(
        pack_kernel,
        name="pack",
        out_shape=jax.ShapeDtypeStruct((8, 128, 1152), BF16),
        grid=(4,),
        in_specs=[rows(4096), rows(4096), rows(1024)],
        out_specs=pl.BlockSpec((8, 32, 1152), lambda i: (0, i, 0)),
        cost_estimate=pl.CostEstimate(flops=0, bytes_accessed=5 << 20, transcendentals=0),
    )(q, g, k)


def choose_kernel(tab_ref, down_ref, up_ref, out_ref):
    for n in range(32):
        row = jnp.minimum(tab_ref[n], 15)
        out_ref[n, :64, :] = down_ref[row]
        out_ref[n, 64:, :] = up_ref[row]


def choose(table, down, up):
    return pl.pallas_call(
        choose_kernel,
        name="choose",
        out_shape=jax.ShapeDtypeStruct((32, ROWS, 128), BF16),
        in_specs=[SMEM, VMEM, VMEM],
        out_specs=VMEM,
        cost_estimate=pl.CostEstimate(flops=0, bytes_accessed=1 << 20, transcendentals=0),
    )(table, down, up)


def pick_kernel(tab_ref, in_ref, out_ref):
    for b in range(32):
        out_ref[b] = in_ref[tab_ref[b]]


def pick(table, fetched):
    return pl.pallas_call(
        pick_kernel,
        name="pick",
        out_shape=jax.ShapeDtypeStruct((32, ROWS, 128), BF16),
        in_specs=[SMEM, VMEM],
        out_specs=VMEM,
        cost_estimate=pl.CostEstimate(flops=0, bytes_accessed=1 << 20, transcendentals=0),
    )(table, fetched)


def long_kernel(tab_ref, own_ref, key_ref, out_ref, keys, acc, sc):
    i = pl.program_id(0)

    @pl.when(i == 0)
    def _():
        acc[...] = jnp.zeros_like(acc)
        for j in range(LONG + 1):
            keys[pl.ds(128 * j, 128), :] = key_ref[tab_ref[10 + j]]

    pos = tab_ref[5 + i]
    last = pos // 2
    base = jnp.where(i == 4, LONG * 128, 0)

    @pl.when(pos >= 0)
    def _():
        own = own_ref[0]
        queries = stack_heads(own[:, :512])
        grads = stack_heads(own[:, 512:1024])

        @pl.when(i == 4)
        def _():
            keys[pl.ds(2176, 128), :] = own[:, 1024:]

        def rows(c):
            return pl.ds(pl.multiple_of(base + c * 256, 256), 256)

        def scores(c):
            return dot_nt(keys[rows(c), :], queries)

        def fold(s):
            return jnp.max(s.reshape(32, 8, 512), axis=0)

        def first(c, top):
            s = scores(c)
            sc[c] = s
            return jnp.maximum(top, fold(s))

        s = scores(last)
        key_at = lax.broadcasted_iota(jnp.int32, (256, 512), 0) + last * 256
        query_at = (lax.broadcasted_iota(jnp.int32, (256, 512), 1) & 127) + pos * 128
        s = jnp.where(key_at <= query_at, s, NEG)
        sc[last] = s
        top = lax.fori_loop(0, last, first, fold(s))
        top = jnp.max(top, axis=0, keepdims=True)

        def second(c, total):
            e = jnp.exp2((sc[c] - top) * FACTOR)
            sc[c] = e
            return total + jnp.sum(e.reshape(32, 8, 512), axis=0)

        total = lax.fori_loop(0, last + 1, second, jnp.zeros((8, 512), F32))
        inverse = 1.0 / jnp.sum(total, axis=0, keepdims=True)

        def third(c, carry):
            p = (sc[c] * inverse).astype(BF16)
            acc[rows(c), :] += dot_nn(p, grads)
            return carry

        lax.fori_loop(0, last + 1, third, 0)

    @pl.when(i == 4)
    def _():
        for j in range(LONG):
            out_ref[tab_ref[27 + j]] = acc[pl.ds(128 * j, 128), :].astype(BF16)
        shared = acc[2048:2176, :].astype(BF16)
        out_ref[4] = shared
        out_ref[17] = shared
        out_ref[18] = acc[2176:, :].astype(BF16)


def long_attention(table, received, keys):
    def whole(*shape):
        return pl.BlockSpec(shape, lambda i, t: (0,) * len(shape))

    return pl.pallas_call(
        long_kernel,
        name="long",
        out_shape=jax.ShapeDtypeStruct((19, 128, 128), BF16),
        grid_spec=pltpu.PrefetchScalarGridSpec(
            num_scalar_prefetch=1,
            grid=(5,),
            in_specs=[
                pl.BlockSpec((1, 128, 1152), lambda i, t: (t[i], 0, 0)),
                whole(20, 128, 128),
            ],
            out_specs=whole(19, 128, 128),
            scratch_shapes=[
                pltpu.VMEM((2304, 128), BF16),
                pltpu.VMEM((2304, 128), F32),
                pltpu.VMEM((8, 256, 512), F32),
            ],
        ),
        compiler_params=pltpu.CompilerParams(vmem_limit_bytes=32 << 20),
        cost_estimate=pl.CostEstimate(
            flops=6 << 30, bytes_accessed=4 << 20, transcendentals=8 << 20
        ),
    )(table, received, keys)


def short_kernel(q_ref, g_ref, k_ref, out_ref):
    key_at = lax.broadcasted_iota(jnp.int32, (128, 512), 0)
    query_at = lax.broadcasted_iota(jnp.int32, (128, 512), 1) & 127
    s = dot_nt(k_ref[...], stack_heads(q_ref[...]))
    s = jnp.where(key_at <= query_at, s, NEG)
    e = jnp.exp2((s - jnp.max(s, axis=0, keepdims=True)) * FACTOR)
    p = (e * (1.0 / jnp.sum(e, axis=0, keepdims=True))).astype(BF16)
    summed = jnp.zeros((128, 128), F32)
    for h in range(4):
        lanes = slice(h * 128, (h + 1) * 128)
        summed += dot_nn(p[:, lanes], g_ref[:, lanes]).astype(BF16).astype(F32)
    out_ref[...] = summed.astype(BF16)


def short_attention(q, g, k):
    wide = pl.BlockSpec((128, 512), lambda i: (0, i))
    thin = pl.BlockSpec((128, 128), lambda i: (0, i))
    return pl.pallas_call(
        short_kernel,
        name="short",
        out_shape=jax.ShapeDtypeStruct((128, 1024), BF16),
        grid=(8,),
        in_specs=[wide, wide, thin],
        out_specs=thin,
        cost_estimate=pl.CostEstimate(
            flops=3 << 30, bytes_accessed=4 << 20, transcendentals=4 << 20
        ),
    )(q, g, k)


def interleave(transposed):
    row = lax.broadcasted_iota(jnp.int32, (512, 512), 0)
    col = lax.broadcasted_iota(jnp.int32, (512, 512), 1)
    if transposed:
        row, col = col, row
    return (col == (row & 7) * 64 + (row >> 3)).astype(BF16)


def low_kernel(x_ref, w_ref, low_ref, up_ref, down):
    for s in range(32):
        down[:, 128 * s : 128 * (s + 1)] = w_ref[s, :64, :]
    low_ref[...] = dot_nt(x_ref[...], down[...]).astype(BF16)
    up_ref[...] = dot_nn(interleave(True), w_ref[:, 64:, :].reshape(512, 128)).astype(BF16)


def low_rank(x, weights):
    return pl.pallas_call(
        low_kernel,
        name="low",
        out_shape=(
            jax.ShapeDtypeStruct((128, 64), BF16),
            jax.ShapeDtypeStruct((512, 128), BF16),
        ),
        in_specs=[VMEM] * 2,
        out_specs=(VMEM, VMEM),
        scratch_shapes=[pltpu.VMEM((64, 4096), BF16)],
        cost_estimate=pl.CostEstimate(flops=1 << 28, bytes_accessed=2 << 20, transcendentals=0),
    )(x, weights)


def terms_kernel(tab_ref, x_ref, low_ref, up_ref, far_ref, own_ref, out_ref):
    low = low_ref[...]
    near, wide = tab_ref[0] > 0, tab_ref[1] > 0
    back = jnp.zeros((128, 64), F32)
    up_terms = []
    for c in range(8):
        lanes = slice(c * 128, (c + 1) * 128)
        value = jnp.where(near, own_ref[:, lanes].astype(F32), 0.0)
        value = (value + jnp.where(wide, far_ref[c].astype(F32), 0.0)).astype(BF16)
        back += dot_nt(value, up_ref[64 * c : 64 * (c + 1), :])
        up_terms.append((2.0 * dot_tn(low, value)).astype(BF16))
    back = (2.0 * back).astype(BF16)
    for s in range(32):
        out_ref[s, :64, :] = dot_tn(back, x_ref[:, 128 * s : 128 * (s + 1)]).astype(BF16)
    mixed = dot_nn(interleave(False), jnp.concatenate(up_terms, axis=0)).astype(BF16)
    out_ref[:, 64:, :] = mixed.reshape(32, 16, 128)


def terms(table, x, low, up, far, own):
    return pl.pallas_call(
        terms_kernel,
        name="terms",
        out_shape=jax.ShapeDtypeStruct((32, ROWS, 128), BF16),
        in_specs=[SMEM] + [VMEM] * 5,
        out_specs=VMEM,
        compiler_params=pltpu.CompilerParams(vmem_limit_bytes=32 << 20),
        cost_estimate=pl.CostEstimate(flops=1 << 29, bytes_accessed=4 << 20, transcendentals=0),
    )(table, x, low, up, far, own)


def gather_sum(tab_ref, in_ref, acc):
    acc[...] = jnp.zeros_like(acc)
    for b in range(32):
        acc[tab_ref[b]] += in_ref[b].astype(F32)


def segment_kernel(tab_ref, in_ref, out_ref, acc):
    gather_sum(tab_ref, in_ref, acc)
    out_ref[...] = acc[...].astype(BF16)


def segment_sum(table, parts):
    rows = pl.BlockSpec((32, 16, 128), lambda i, t: (0, i, 0))
    return pl.pallas_call(
        segment_kernel,
        name="segments",
        out_shape=jax.ShapeDtypeStruct((32, ROWS, 128), BF16),
        grid_spec=pltpu.PrefetchScalarGridSpec(
            num_scalar_prefetch=1,
            grid=(ROWS // 16,),
            in_specs=[rows],
            out_specs=rows,
            scratch_shapes=[pltpu.VMEM((32, 16, 128), F32)],
        ),
    )(table, parts)


def adapter_kernel(tab_ref, in_ref, down_ref, up_ref, acc):
    gather_sum(tab_ref, in_ref, acc)
    down_ref[...] = acc[:16, :64, :]
    for r in range(2):
        for c in range(8):
            up_ref[:, r, 128 * c : 128 * (c + 1)] = acc[:16, 64 + 8 * r + c, :]


def adapter_sum(table, parts):
    return pl.pallas_call(
        adapter_kernel,
        name="adapters",
        out_shape=(
            jax.ShapeDtypeStruct((16, 64, 128), F32),
            jax.ShapeDtypeStruct((16, 2, 1024), F32),
        ),
        in_specs=[SMEM, VMEM],
        out_specs=(VMEM, VMEM),
        scratch_shapes=[pltpu.VMEM((24, ROWS, 128), F32)],
    )(table, parts)


def exchange(value, axis, groups=None):
    return lax.all_to_all(value, axis, 0, 0, axis_index_groups=groups, tiled=True)


def row_shift(value, step):
    pairs = [
        (8 * x + 2 * q + p, 8 * x + 2 * ((q + step) % 4) + p)
        for x in range(4)
        for q in range(4)
        for p in range(2)
    ]
    return lax.ppermute(value, "seq", pairs)


def local(x, q, k, g, down_weight, up_weight, seg_adapter, seg_blocks, row_index):
    group = lax.axis_index("grp")
    place = lax.axis_index("seq")
    residents = down_weight.shape[0]
    i32 = jnp.int32

    received = exchange(pack(q, g, k), "seq", COLUMN)
    own_value = short_attention(q, g, k)

    ids = jnp.arange(row_index.shape[0], dtype=i32)
    slot_of = jnp.sum(jnp.where(seg_adapter[:, :, None] == ids, row_index, 0), axis=2)
    owner = slot_of // residents
    inner = slot_of % residents
    order = jnp.arange(16, dtype=i32)
    earlier = order[:, None] > order[None, :]
    rank = jnp.sum(((owner[:, :, None] == owner[:, None, :]) & earlier).astype(i32), axis=2)
    mine = owner == group
    target = jnp.stack(
        [jnp.min(jnp.where(mine & (rank == c), inner, 16), axis=1) for c in range(CAP)], axis=1
    ).reshape(32)

    counts = lax.dynamic_index_in_dim(seg_blocks, group, 0, keepdims=False)
    ends = jnp.sum(jnp.where(order[:, None] >= order[None, :], counts[None, :], 0), axis=1)
    starts = ends - counts
    blocks = jnp.arange(32, dtype=i32)
    inside = (blocks[:, None] >= starts[None, :]) & (blocks[:, None] < ends[None, :])
    own_places = lax.dynamic_index_in_dim(owner * CAP + rank, group, 0, keepdims=False)
    block_place = jnp.sum(jnp.where(inside, own_places[None, :], 0), axis=1)
    long_start = jnp.sum(jnp.where(counts == LONG, starts, 0))
    pair_start = jnp.sum(jnp.where(counts == 2, starts, 0))
    counted = jnp.sum(jnp.where(inside, counts[None, :], 0), axis=1)
    counted = lax.dynamic_index_in_dim(counted, place, 0)
    flags = jnp.concatenate([(counted == 1) | (place == pair_start), counted > 1]).astype(i32)

    y2 = (place % 8) // 2
    four = jnp.arange(4, dtype=i32)
    residue = 8 * (four // 2) + 2 * y2 + four % 2
    source = jnp.where(residue < long_start, four + 4, four)
    pair = pair_start + jnp.arange(2, dtype=i32)
    pair_member = pair // 8 * 2 + pair % 2
    pair_row = (pair % 8) // 2
    sixteen = (long_start + order) % 16
    within = sixteen // 8 * 2 + sixteen % 2
    home = (sixteen % 8) // 2
    up_row = (home - y2) % 4
    table = jnp.concatenate(
        [
            source,
            pair_member[1:],
            (residue - long_start) % 16,
            jnp.where(pair_row[1:] == y2, 1, -1),
            5 * home + within,
            5 * pair_row[:1] + 4,
            4 * up_row + (up_row > 0) + within,
        ]
    )
    members = jnp.arange(8, dtype=i32)[:, None, None]
    is_long = jnp.tile(source, 2)[:, None, None] == members
    is_first = (pair_member[0] == members) & (pair_row[0] == y2)

    halves = received.reshape(2, 4, 128, 1152)[:, :, :, 1024:]
    long_keys = jnp.where((source > 3)[:, None, None], halves[1], halves[0])
    pair_key = lax.dynamic_slice(received, (pair_member[0], 0, 1024), (1, 128, 128))
    long_keys = jnp.concatenate([long_keys, pair_key], axis=0)

    chosen = choose(target, down_weight, up_weight.reshape(residents, 16, 128))
    chosen, long_keys, own_value, table, block_place, flags = lax.optimization_barrier(
        (chosen, long_keys, own_value, table, block_place, flags)
    )
    fetched = exchange(chosen, "grp")
    keys = lax.all_gather(long_keys, "seq", axis=0, tiled=True, axis_index_groups=ROW)

    picked, keys = lax.optimization_barrier((pick(block_place, fetched), keys))
    weights = exchange(picked, "seq")
    partial = long_attention(table, received, keys)
    last = row_shift(partial[13:18], 3)
    head_value = (
        partial[:4].astype(F32)
        + row_shift(partial[5:9], 1).astype(F32)
        + row_shift(partial[9:13], 2).astype(F32)
        + last[:4].astype(F32)
    ).astype(BF16)
    first_value = partial[4] + last[4]
    head_value = jnp.where(
        is_long,
        jnp.concatenate([head_value, head_value], axis=0),
        jnp.where(is_first, first_value, partial[18]),
    )
    head_value, weights = lax.optimization_barrier((head_value, weights))
    far = exchange(head_value, "seq", COLUMN)

    parts = exchange(terms(flags, x, *low_rank(x, weights), far, own_value), "seq")
    sums = exchange(segment_sum(block_place, parts), "grp")
    return adapter_sum(target, sums)


def solution(mesh):
    rows = P(("grp", "seq"), None)
    return jax.shard_map(
        local,
        mesh=mesh,
        in_specs=(rows,) * 4 + (P("grp", None, "seq"), P("grp", "seq", None)) + (P(),) * 3,
        out_specs=(P("grp", None, "seq"), P("grp", "seq", None)),
        check_vma=False,
    )
```
